128 devices in a mesh: gx: 4 (over z), gy: 4 (over y), gz: 8 (over x, core).
Axes of the slice: x: 4, y: 4, z: 4, core: 2. Of those that a mesh axis runs over, the one named last changes fastest.
Arguments:
- basis: float32 [4, 64, 64, 64, 512], P(None, None, 'gz', 'gx', 'gy'), may hold values from -1000 to 1000
- stand_id: int32 [64, 64, 512], P('gz', 'gx', 'gy'), may hold values from 0 to 63
- drag_table: float32 [64], replicated, may hold values from 0.5 to 8
- stand_mask: int32 [64], replicated, may hold values 0 or 1
Outputs:
- fresh_block: float32 [64, 64, 64, 512], P(None, 'gz', 'gx', 'gy')
- projections: float32 [4, 64, 64], replicated
- factor: float32 [64, 64], replicated
The draws below stay inside these ranges and needn't reach their ends.
All inputs are finite; a program needn't handle non-finite values.
Results may differ from the reference program's by a relative error of at most 0.00085.
Values sent between devices are 32-bit elements; how exact they have to be, the bound alone decides.
No kernel may reach another device: no remote copies, remote signals or barrier semaphores. Data moves between devices by JAX's collectives and lax.ppermute only.
A program may use at most 128 MiB of HBM per device.

```python
import math
import jax
import jax.numpy as jnp
from jax import lax

K = 64
NB = 4
STANDS = 64
NX = 64
NY = 64
NZ = 512


def draw_basis(key, part):
    keys = jax.random.split(key, 3)
    shape_all = (NB, K, NX, NY, NZ)
    common = jnp.clip(jax.random.normal(keys[0], (K, NX, NY, NZ), jnp.float32), -4.0, 4.0)
    own_part = jnp.clip(jax.random.normal(keys[1], shape_all, jnp.float32), -4.0, 4.0)
    power = 1.0
    roughness = jnp.exp(jax.random.uniform(keys[2], (1, 1, NX, NY, NZ), jnp.float32, -1.15, 1.15))
    ramp_x = 0.5 + (jnp.arange(NX, dtype=jnp.float32) + 0.5) / NX
    ramp_y = 0.5 + (jnp.arange(NY, dtype=jnp.float32) + 0.5) / NY
    ramp_z = 0.5 + (jnp.arange(NZ, dtype=jnp.float32) + 0.5) / NZ
    ramp = (ramp_x[:, None, None] * ramp_y[None, :, None] * ramp_z[None, None, :]) ** power
    mixed = (0.6 * common[None] + 0.8 * own_part) * roughness * ramp[None, None]
    return mixed.astype(jnp.float32)


def set_ends(values, rng, least, largest):
    spot = [jax.random.randint(jax.random.fold_in(rng, axis), (), 0, length) for axis, length in enumerate(values.shape)]
    widest = values.shape.index(max(values.shape))
    neighbour = spot[:widest] + [(spot[widest] + 1) % values.shape[widest]] + spot[widest + 1:]
    return values.at[tuple(spot)].set(least).at[tuple(neighbour)].set(largest)


def setup_inputs(seed: int = 0) -> dict:
    splits = jax.random.split(jax.random.key(seed), 5)
    basis = draw_basis(jax.random.fold_in(splits[4], 71), 0)
    stand_id = set_ends(jax.random.randint(splits[1], (NX, NY, NZ), 0, STANDS), jax.random.fold_in(splits[1], 1), 0, STANDS - 1).astype(jnp.int32)
    drag_table = jnp.clip(jnp.exp(jax.random.uniform(splits[2], (STANDS,), jnp.float32, math.log(0.5), math.log(8.0))), 0.5, 8.0)
    stand_mask = set_ends((jax.random.randint(splits[3], (STANDS,), 0, 2) < 1).astype(jnp.int32), jax.random.fold_in(splits[3], 1), 0, 1)
    return {"basis": basis, "stand_id": stand_id, "drag_table": drag_table, "stand_mask": stand_mask}


advection = (0.3, 0.2, 0.1)

def adjoint_apply(field_block, cell_drag):
    padded = jnp.pad(field_block, ((0, 0), (1, 1), (1, 1), (1, 1)))
    centre_field = padded[:, 1:-1, 1:-1, 1:-1]
    summed = (6.0 + cell_drag) * centre_field
    upper_sides = (padded[:, 2:, 1:-1, 1:-1], padded[:, 1:-1, 2:, 1:-1], padded[:, 1:-1, 1:-1, 2:])
    lower_sides = (padded[:, :-2, 1:-1, 1:-1], padded[:, 1:-1, :-2, 1:-1], padded[:, 1:-1, 1:-1, :-2])
    for weight, upper_side, lower_side in zip(advection, upper_sides, lower_sides):
        summed = summed - (1.0 + weight) * upper_side - (1.0 - weight) * lower_side
    return summed

def reference(basis, stand_id, drag_table, stand_mask):
    per_stand = drag_table * stand_mask.astype(jnp.float32)
    cell_drag = per_stand[stand_id]
    newest = basis[NB - 1]
    applied = adjoint_apply(newest, cell_drag)
    ncells = NX * NY * NZ
    flat_basis = basis.reshape(NB * K, ncells)
    flat_applied = applied.reshape(K, ncells)
    dims_rows = (((1,), (1,)), ((), ()))
    coeffs = lax.dot_general(flat_basis.astype(jnp.float32), flat_applied.astype(jnp.float32), dims_rows, precision=lax.Precision.HIGHEST, preferred_element_type=jnp.float32) / ncells
    residual = flat_applied - lax.dot_general(coeffs.astype(jnp.float32), flat_basis.astype(jnp.float32), (((0,), (0,)), ((), ())), precision=lax.Precision.HIGHEST, preferred_element_type=jnp.float32)
    gram_block = lax.dot_general(residual.astype(jnp.float32), residual.astype(jnp.float32), dims_rows, precision=lax.Precision.HIGHEST, preferred_element_type=jnp.float32) / ncells
    chol_lower = jnp.linalg.cholesky(gram_block)
    fresh_block = jax.scipy.linalg.solve_triangular(chol_lower, residual, lower=True)
    return (fresh_block.reshape(K, NX, NY, NZ), coeffs.reshape(NB, K, K), chol_lower.T)
```

```python
import jax
import jax.numpy as jnp
from jax import lax
from jax.sharding import PartitionSpec as P

advection = (0.3, 0.2, 0.1)
ROW_DIMS = (((1,), (1,)), ((), ()))
LEAD_DIMS = (((0,), (0,)), ((), ()))


def exchange(value, axis, mask):
    pairs = [(source, source ^ mask) for source in range(lax.axis_size(axis))]
    return lax.ppermute(value, axis, pairs)


def quad_sum(value, axis, masks):
    parts = [exchange(value, axis, mask) for mask in masks]
    return (value + parts[0]) + (parts[1] + parts[2])


def total(value):
    core = lax.axis_index("gz") % 2
    half = value.shape[0] // 2
    keep = lax.dynamic_slice_in_dim(value, core * half, half, 0)
    give = lax.dynamic_slice_in_dim(value, (1 - core) * half, half, 0)
    part = keep + exchange(give, "gz", 1)
    part = quad_sum(part, "gz", (2, 4, 6))
    part = quad_sum(part, "gy", (1, 2, 3))
    part = quad_sum(part, "gx", (1, 2, 3))
    other = exchange(part, "gz", 1)
    first = jnp.where(core == 0, part, other)
    second = jnp.where(core == 0, other, part)
    return jnp.concatenate([first, second])


def neighbours(block, axis, dim):
    count = lax.axis_size(axis)
    forward = [(i, i + 1) for i in range(count - 1)]
    backward = [(target, source) for source, target in forward]
    last = lax.slice_in_dim(block, block.shape[dim] - 1, None, axis=dim)
    first = lax.slice_in_dim(block, 0, 1, axis=dim)
    low = lax.ppermute(last, axis, forward)
    high = lax.ppermute(first, axis, backward)
    upper = jnp.concatenate([lax.slice_in_dim(block, 1, None, axis=dim), high], axis=dim)
    lower = jnp.concatenate([low, lax.slice_in_dim(block, 0, block.shape[dim] - 1, axis=dim)], axis=dim)
    return upper, lower


def contract(left, right, numbers):
    return lax.dot_general(
        left, right, numbers, precision=lax.Precision.HIGHEST, preferred_element_type=jnp.float32
    )


def body(basis, stand_id, drag_table, stand_mask):
    blocks, columns = basis.shape[:2]
    local_shape = stand_id.shape
    cells = local_shape[0] * local_shape[1] * local_shape[2]
    ncells = cells * lax.axis_size("gx") * lax.axis_size("gy") * lax.axis_size("gz")
    stands = drag_table.shape[0]
    per_stand = drag_table * stand_mask.astype(jnp.float32)
    onehot = (jnp.arange(stands, dtype=jnp.int32)[:, None] == stand_id.reshape(1, cells)).astype(jnp.float32)
    cell_drag = jnp.dot(
        per_stand[None, :], onehot, precision=lax.Precision.HIGHEST, preferred_element_type=jnp.float32
    ).reshape(local_shape)
    newest = basis[blocks - 1]
    applied = (6.0 + cell_drag) * newest
    for weight, axis, dim in zip(advection, ("gz", "gx", "gy"), (1, 2, 3)):
        upper, lower = neighbours(newest, axis, dim)
        applied = applied - (1.0 + weight) * upper - (1.0 - weight) * lower
    flat_applied = applied.reshape(columns, cells)
    flat_basis = basis.reshape(blocks * columns, cells)
    coeffs = total(contract(flat_basis, flat_applied, ROW_DIMS) / ncells)
    residual = flat_applied - contract(coeffs, flat_basis, LEAD_DIMS)
    gram = total(contract(residual, residual, ROW_DIMS) / ncells)
    chol_lower = jnp.linalg.cholesky(gram)
    fresh_block = jax.scipy.linalg.solve_triangular(chol_lower, residual, lower=True)
    return (
        fresh_block.reshape(applied.shape),
        coeffs.reshape(blocks, columns, columns),
        chol_lower.T,
    )


def solution(mesh):
    placed = (P(None, None, "gz", "gx", "gy"), P("gz", "gx", "gy"), P(), P())
    return jax.shard_map(
        body,
        mesh=mesh,
        in_specs=placed,
        out_specs=(P(None, "gz", "gx", "gy"), P(), P()),
        check_vma=False,
    )
```

```python
import jax
import jax.numpy as jnp
from jax import lax
from jax.experimental import pallas as pl
from jax.experimental.pallas import tpu as pltpu
from jax.sharding import PartitionSpec as P

advection = (0.3, 0.2, 0.1)
ROW_DIMS = (((1,), (1,)), ((), ()))
MAT_DIMS = (((1,), (0,)), ((), ()))
LANES = 128
F32 = jnp.float32
BF16 = jnp.bfloat16


def exchange(value, axis, mask):
    pairs = [(source, source ^ mask) for source in range(lax.axis_size(axis))]
    return lax.ppermute(value, axis, pairs)


def quad_sum(value, axis, masks):
    parts = [exchange(value, axis, mask) for mask in masks]
    return (value + parts[0]) + (parts[1] + parts[2])


def total(value):
    core = lax.axis_index("gz") % 2
    half = value.shape[0] // 2
    keep = lax.dynamic_slice_in_dim(value, core * half, half, 0)
    give = lax.dynamic_slice_in_dim(value, (1 - core) * half, half, 0)
    part = keep + exchange(give, "gz", 1)
    part = quad_sum(part, "gz", (2, 4, 6))
    part = quad_sum(part, "gy", (1, 2, 3))
    part = quad_sum(part, "gx", (1, 2, 3))
    other = exchange(part, "gz", 1)
    first = jnp.where(core == 0, part, other)
    second = jnp.where(core == 0, other, part)
    return jnp.concatenate([first, second])


def exact(left, right, numbers=MAT_DIMS):
    return lax.dot_general(left, right, numbers, precision=lax.Precision.HIGHEST, preferred_element_type=F32)


def narrow(left, right, numbers=MAT_DIMS):
    return lax.dot_general(left, right, numbers, preferred_element_type=F32)


def split(value):
    high = value.astype(BF16)
    return high, (value - high.astype(F32)).astype(BF16)


def faces(newest, sx, sy, blocks):
    columns = newest.shape[1] // (sx * sy)
    step = 16

    def kernel(src, x_first, x_last, y_first, y_last, z_first, z_last):
        flat = src.at[0]
        lane = lax.broadcasted_iota(jnp.int32, (step, LANES), 1)
        first = jnp.zeros((step, LANES), F32)
        last = jnp.zeros((step, LANES), F32)
        for x in range(sx):
            for y in range(sy):
                cell = x * sy + y
                row = flat[pl.ds(cell, step, stride=sx * sy), :]
                if x == 0:
                    x_first[y] = row
                if x == sx - 1:
                    x_last[y] = row
                if y == 0:
                    y_first[x] = row
                if y == sy - 1:
                    y_last[x] = row
                turned = pltpu.roll(row, cell, 1) if cell else row
                first = jnp.where(lane == cell, turned, first)
                last = jnp.where(lane == (cell - 1) % LANES, turned, last)
        z_first[...] = first
        z_last[...] = last

    grid = columns // step
    return pl.pallas_call(
        kernel,
        grid=(grid,),
        in_specs=[pl.BlockSpec((1, step * sx * sy, LANES), lambda i: (blocks - 1, i, 0))],
        out_specs=[
            pl.BlockSpec((sy, step, LANES), lambda i: (0, i, 0)),
            pl.BlockSpec((sy, step, LANES), lambda i: (0, i, 0)),
            pl.BlockSpec((sx, step, LANES), lambda i: (0, i, 0)),
            pl.BlockSpec((sx, step, LANES), lambda i: (0, i, 0)),
            pl.BlockSpec((step, LANES), lambda i: (i, 0)),
            pl.BlockSpec((step, LANES), lambda i: (i, 0)),
        ],
        out_shape=[
            jax.ShapeDtypeStruct((sy, columns, LANES), F32),
            jax.ShapeDtypeStruct((sy, columns, LANES), F32),
            jax.ShapeDtypeStruct((sx, columns, LANES), F32),
            jax.ShapeDtypeStruct((sx, columns, LANES), F32),
            jax.ShapeDtypeStruct((columns, LANES), F32),
            jax.ShapeDtypeStruct((columns, LANES), F32),
        ],
        name="faces",
    )(newest)


def local_part(basis, stand_id, drag_table, stand_mask, sx, sy, columns):
    rows = basis.shape[0]
    width = sy * LANES
    stands = drag_table.shape[0]

    def kernel(table, mask, src, ids, halves, applied, own, slabs, acc):
        step = pl.program_id(0)

        @pl.when(step == 0)
        def _():
            slabs[0] = jnp.zeros((columns, width), F32)
            slabs[sx + 1] = jnp.zeros((columns, width), F32)
            acc[...] = jnp.zeros_like(acc)

        @pl.when(step < sx)
        def _():
            flat = src.reshape(rows * sy, LANES)
            for y in range(sy):
                cols = pl.ds(y * LANES, LANES)
                value = flat[pl.ds(y, rows, stride=sy), :]
                high, low = split(value)
                halves[0, 0:rows, cols] = high
                halves[0, rows : 2 * rows, cols] = low
                slabs[step + 1, :, cols] = value[rows - columns :, :]
            acc[...] += narrow(halves[0], halves[0, 0:rows, :], ROW_DIMS)

        @pl.when(step > 0)
        def _():
            lane = lax.broadcasted_iota(jnp.int32, (1, LANES), 1)
            z_up = jnp.where(lane == LANES - 1, 0.0, 1.0 + advection[2])
            z_down = jnp.where(lane == 0, 0.0, 1.0 - advection[2])
            stand = ids[0]
            drag = jnp.zeros(stand.shape, F32)
            for s in range(stands):
                drag = jnp.where(stand == s, table[s] * mask[s].astype(F32), drag)
            for y in range(sy):
                cols = pl.ds(y * LANES, LANES)
                centre = slabs[step, :, cols]
                out = (6.0 + drag[y : y + 1, :]) * centre
                out = out - (1.0 + advection[0]) * slabs[step + 1, :, cols]
                out = out - (1.0 - advection[0]) * slabs[step - 1, :, cols]
                if y < sy - 1:
                    out = out - (1.0 + advection[1]) * slabs[step, :, pl.ds((y + 1) * LANES, LANES)]
                if y > 0:
                    out = out - (1.0 - advection[1]) * slabs[step, :, pl.ds((y - 1) * LANES, LANES)]
                out = out - z_up * pltpu.roll(centre, LANES - 1, 1)
                out = out - z_down * pltpu.roll(centre, 1, 1)
                applied[0, :, cols] = out

        @pl.when(step == sx)
        def _():
            cross = acc[rows : 2 * rows, :]
            own[...] = acc[0:rows, :] + cross + cross.T

    last = sx - 1
    return pl.pallas_call(
        kernel,
        grid=(sx + 1,),
        in_specs=[
            pl.BlockSpec(memory_space=pltpu.SMEM),
            pl.BlockSpec(memory_space=pltpu.SMEM),
            pl.BlockSpec((rows, 1, sy, LANES), lambda i: (0, jnp.minimum(i, last), 0, 0)),
            pl.BlockSpec((1, sy, LANES), lambda i: (jnp.maximum(i - 1, 0), 0, 0)),
        ],
        out_specs=[
            pl.BlockSpec((1, 2 * rows, width), lambda i: (jnp.minimum(i, last), 0, 0)),
            pl.BlockSpec((1, columns, width), lambda i: (jnp.maximum(i - 1, 0), 0, 0)),
            pl.BlockSpec((rows, rows), lambda i: (0, 0)),
        ],
        out_shape=[
            jax.ShapeDtypeStruct((sx, 2 * rows, width), BF16),
            jax.ShapeDtypeStruct((sx, columns, width), F32),
            jax.ShapeDtypeStruct((rows, rows), F32),
        ],
        scratch_shapes=[
            pltpu.VMEM((sx + 2, columns, width), F32),
            pltpu.VMEM((2 * rows, rows), F32),
        ],
        compiler_params=pltpu.CompilerParams(vmem_limit_bytes=56 * 2**20),
        name="local_part",
    )(drag_table, stand_mask, basis, stand_id)


def products(halves, applied, own, halos, scale):
    sx, rows2, width = halves.shape
    rows = rows2 // 2
    columns = applied.shape[1]
    sy = width // LANES
    half = rows // 2

    def kernel(halves, applied, own, x_low, x_high, y_low, y_high, z_low, z_high, out, packed, slab, acc, acc2):
        step = pl.program_id(0)

        @pl.when(step == 0)
        def _():
            acc[...] = jnp.zeros_like(acc)
            acc2[...] = jnp.zeros_like(acc2)

        slab[...] = applied[0]

        @pl.when(step == 0)
        def _():
            for y in range(sy):
                slab[:, pl.ds(y * LANES, LANES)] -= (1.0 - advection[0]) * x_low[y]

        @pl.when(step == sx - 1)
        def _():
            for y in range(sy):
                slab[:, pl.ds(y * LANES, LANES)] -= (1.0 + advection[0]) * x_high[y]

        lane = lax.broadcasted_iota(jnp.int32, (1, LANES), 1)
        z_up = jnp.where(lane == LANES - 1, 1.0 + advection[2], 0.0)
        z_down = jnp.where(lane == 0, 1.0 - advection[2], 0.0)
        base = step * sy
        low = pltpu.roll(z_low[...], (LANES + 1 - base) % LANES, 1)
        high = pltpu.roll(z_high[...], (LANES - base) % LANES, 1)
        for y in range(sy):
            cols = pl.ds(y * LANES, LANES)
            value = slab[:, cols]
            if y == 0:
                value = value - (1.0 - advection[1]) * y_low[step]
            if y == sy - 1:
                value = value - (1.0 + advection[1]) * y_high[step]
            shift = (LANES - y) % LANES
            value = value - z_down * (pltpu.roll(low, shift, 1) if shift else low)
            shift = (LANES - 1 - y) % LANES
            value = value - z_up * pltpu.roll(high, shift, 1)
            top, rest = split(value)
            out[0, 0:columns, cols] = top
            out[0, columns : 2 * columns, cols] = rest
        @pl.when(step < sx)
        def _():
            acc[...] += narrow(halves[0], out[0], ROW_DIMS)
            acc2[...] += narrow(out[0], out[0], ROW_DIMS)

        @pl.when(step == sx - 1)
        def _():
            mixed = acc[0:rows, :] + acc[rows:rows2, :]
            coeffs = (mixed[:, 0:columns] + mixed[:, columns:]) * scale
            square = acc2[0:columns, :] + acc2[columns:, :]
            square = (square[:, 0:columns] + square[:, columns:]) * scale
            corner = own[half:, half:] * scale
            row = lax.broadcasted_iota(jnp.int32, (half, half), 0)
            col = lax.broadcasted_iota(jnp.int32, (half, half), 1)
            packed[0:half, :] = own[0:half, half:] * scale
            packed[half:rows, :] = jnp.where(row <= col, own[0:half, 0:half] * scale, corner)
            packed[rows : rows + half, 0:columns] = coeffs[0:half, :]
            packed[rows : rows + half, columns:] = coeffs[half:, :]
            packed[rows + half : rows + half + columns, :] = jnp.zeros((columns, LANES), F32)
            packed[rows + half : rows + half + columns, 0:columns] = square
            diag = jnp.sum(jnp.where(row == col, corner, 0.0), axis=0, keepdims=True)
            packed[rows + half + columns :, :] = jnp.broadcast_to(diag, (16, LANES))

    whole = [pl.BlockSpec(h.shape, lambda i, n=h.ndim: (0,) * n) for h in halos]
    size = rows + half + columns + 16
    return pl.pallas_call(
        kernel,
        grid=(sx,),
        in_specs=[
            pl.BlockSpec((1, rows2, width), lambda i: (i, 0, 0)),
            pl.BlockSpec((1, columns, width), lambda i: (i, 0, 0)),
            pl.BlockSpec((rows, rows), lambda i: (0, 0)),
            *whole,
        ],
        out_specs=[
            pl.BlockSpec((1, 2 * columns, width), lambda i: (i, 0, 0)),
            pl.BlockSpec((size, LANES), lambda i: (0, 0)),
        ],
        out_shape=[
            jax.ShapeDtypeStruct((sx, 2 * columns, width), BF16),
            jax.ShapeDtypeStruct((size, LANES), F32),
        ],
        scratch_shapes=[
            pltpu.VMEM((columns, width), F32),
            pltpu.VMEM((rows2, 2 * columns), F32),
            pltpu.VMEM((2 * columns, 2 * columns), F32),
        ],
        compiler_params=pltpu.CompilerParams(vmem_limit_bytes=56 * 2**20),
        name="products",
    )(halves, applied, own, *halos)


def finish(packed, halves, applied):
    sx, rows2, width = halves.shape
    rows = rows2 // 2
    columns = applied.shape[1] // 2
    sy = width // LANES
    half = rows // 2

    def kernel(packed, halves, applied, fresh, coeffs_out, factor_out, basis, block, staged, sem_in, sem_out):
        copies = []
        for x in range(sx):
            copies.append(
                (
                    pltpu.make_async_copy(halves.at[x], basis.at[x], sem_in.at[0, x]),
                    pltpu.make_async_copy(applied.at[x], block.at[x], sem_in.at[1, x]),
                )
            )
            for copy in copies[-1]:
                copy.start()
        row = lax.broadcasted_iota(jnp.int32, (half, half), 0)
        col = lax.broadcasted_iota(jnp.int32, (half, half), 1)
        mixed = packed[half:rows, :]
        upper = jnp.where(row < col, mixed, 0.0)
        s11 = upper + upper.T + jnp.where(row == col, mixed, 0.0)
        lower = jnp.where(row > col, mixed, 0.0)
        diag = packed[rows + half + columns : rows + half + columns + 1, :]
        s22 = lower + lower.T + jnp.where(row == col, diag, 0.0)
        s12 = packed[0:half, :]
        coeffs = jnp.concatenate(
            [packed[rows : rows + half, 0:columns], packed[rows : rows + half, columns:]], axis=0
        )
        coeffs_out[...] = coeffs
        turned = coeffs.T
        left, right = turned[:, 0:half], turned[:, half:]
        first = exact(left, s11) + exact(right, s12, ROW_DIMS) - 2.0 * left
        second = exact(left, s12) + exact(right, s22) - 2.0 * right
        gram = packed[rows + half : rows + half + columns, 0:columns]
        gram = gram + exact(first, left, ROW_DIMS) + exact(second, right, ROW_DIMS)
        gram = 0.5 * (gram + gram.T)
        eye = (
            lax.broadcasted_iota(jnp.int32, (columns, columns), 0)
            == lax.broadcasted_iota(jnp.int32, (columns, columns), 1)
        ).astype(F32)
        work = jnp.concatenate([gram, eye], axis=1)
        done = []
        below = work
        for j in range(columns):
            pivot = below[0:1, j : j + 1]
            inverse = lax.rsqrt(pivot)
            inverse = inverse * (1.5 - 0.5 * pivot * inverse * inverse)
            scaled = below[0:1, :] * inverse
            done.append(scaled)
            if j < columns - 1:
                below = below[1:, :] - (below[1:, j : j + 1] * inverse) * scaled
        solved = jnp.concatenate(done, axis=0)
        factor = solved[:, 0:columns]
        tri_row = lax.broadcasted_iota(jnp.int32, (columns, columns), 0)
        tri_col = lax.broadcasted_iota(jnp.int32, (columns, columns), 1)
        factor_out[...] = jnp.where(tri_row <= tri_col, factor, 0.0)
        inv = solved[:, columns:]
        back = -exact(inv, turned)
        inv_top, inv_rest = split(inv)
        back_top, back_rest = split(back)
        on_top = jnp.concatenate([back_top, back_rest], axis=0)
        inv_both = jnp.concatenate([inv_top, inv_rest], axis=0)
        outs = []
        for x in range(sx):
            for copy in copies[x]:
                copy.wait()
            big = narrow(on_top, basis[x, 0:rows, :])
            value = big[0:columns] + big[columns:] + narrow(back_top, basis[x, rows:, :])
            big = narrow(inv_both, block[x, 0:columns, :])
            value = value + (big[0:columns] + big[columns:]) + narrow(inv_top, block[x, columns:, :])
            slot = x % 2
            if x >= 2:
                outs[x - 2].wait()
            target = staged.at[slot].reshape(columns * sy, LANES)
            for y in range(sy):
                target[pl.ds(y, columns, stride=sy), :] = value[:, y * LANES : (y + 1) * LANES]
            outs.append(pltpu.make_async_copy(staged.at[slot], fresh.at[:, x], sem_out.at[slot]))
            outs[x].start()
        outs[sx - 2].wait()
        outs[sx - 1].wait()

    vmem = pl.BlockSpec(memory_space=pltpu.VMEM)
    anywhere = pl.BlockSpec(memory_space=pl.ANY)
    return pl.pallas_call(
        kernel,
        in_specs=[vmem, anywhere, anywhere],
        out_specs=[anywhere, vmem, vmem],
        out_shape=[
            jax.ShapeDtypeStruct((columns, sx, sy, LANES), F32),
            jax.ShapeDtypeStruct((rows, columns), F32),
            jax.ShapeDtypeStruct((columns, columns), F32),
        ],
        scratch_shapes=[
            pltpu.VMEM(halves.shape, BF16),
            pltpu.VMEM(applied.shape, BF16),
            pltpu.VMEM((2, columns, sy, LANES), F32),
            pltpu.SemaphoreType.DMA((2, sx)),
            pltpu.SemaphoreType.DMA((2,)),
        ],
        compiler_params=pltpu.CompilerParams(vmem_limit_bytes=56 * 2**20),
        name="finish",
    )(packed, halves, applied)


def send_on(value, axis, forward):
    count = lax.axis_size(axis)
    pairs = [(i, i + 1) if forward else (i + 1, i) for i in range(count - 1)]
    return lax.ppermute(value, axis, pairs)


def body(basis, stand_id, drag_table, stand_mask):
    blocks, columns, sx, sy, sz = basis.shape
    ncells = sx * sy * sz * lax.axis_size("gx") * lax.axis_size("gy") * lax.axis_size("gz")
    x_first, x_last, y_first, y_last, z_first, z_last = faces(
        basis.reshape(blocks, columns * sx * sy, sz), sx, sy, blocks
    )
    halos = (
        send_on(x_last, "gz", True),
        send_on(x_first, "gz", False),
        send_on(y_last, "gx", True),
        send_on(y_first, "gx", False),
        send_on(z_last, "gy", True),
        send_on(z_first, "gy", False),
    )
    halves, applied, own = local_part(
        basis.reshape(blocks * columns, sx, sy, sz), stand_id, drag_table, stand_mask, sx, sy, columns
    )
    applied, packed = products(halves, applied, own, halos, 1.0 / ncells)
    fresh_block, coeffs, factor = finish(total(packed), halves, applied)
    return fresh_block, coeffs.reshape(blocks, columns, columns), factor


def solution(mesh):
    placed = (P(None, None, "gz", "gx", "gy"), P("gz", "gx", "gy"), P(), P())
    return jax.shard_map(
        body,
        mesh=mesh,
        in_specs=placed,
        out_specs=(P(None, "gz", "gx", "gy"), P(), P()),
        check_vma=False,
    )
```

```python
import jax
import jax.numpy as jnp
from jax import lax
from jax.experimental import pallas as pl
from jax.experimental.pallas import tpu as pltpu
from jax.sharding import PartitionSpec as P

advection = (0.3, 0.2, 0.1)
ROW_DIMS = (((1,), (1,)), ((), ()))
MAT_DIMS = (((1,), (0,)), ((), ()))
LANES = 128
F32 = jnp.float32
BF16 = jnp.bfloat16


def exchange(value, axis, mask):
    pairs = [(source, source ^ mask) for source in range(lax.axis_size(axis))]
    return lax.ppermute(value, axis, pairs)


def quad_sum(value, axis, masks):
    parts = [exchange(value, axis, mask) for mask in masks]
    return (value + parts[0]) + (parts[1] + parts[2])


def total(keep, give):
    part = keep + exchange(give, "gz", 1)
    part = quad_sum(part, "gz", (2, 4, 6))
    part = quad_sum(part, "gy", (1, 2, 3))
    part = quad_sum(part, "gx", (1, 2, 3))
    return part, exchange(part, "gz", 1)


def exact(left, right, numbers=MAT_DIMS):
    return lax.dot_general(left, right, numbers, precision=lax.Precision.HIGHEST, preferred_element_type=F32)


def narrow(left, right, numbers=MAT_DIMS):
    return lax.dot_general(left, right, numbers, preferred_element_type=F32)


def split(value):
    high = value.astype(BF16)
    return high, (value - high.astype(F32)).astype(BF16)


def resident(value):
    return pltpu.with_memory_space_constraint(value, pltpu.VMEM)


def even_here(axis, shape):
    return jnp.full(shape, lax.axis_index(axis) % 2, jnp.int32) == 0


def local_part(basis, stand_id, drag_table, stand_mask):
    rows, sx, sy, _ = basis.shape
    columns = rows // 4
    cells = sx * sy
    stands = drag_table.shape[0]
    slots = 3

    def kernel(table_in, mask_in, ids_in, src, halves, applied, own, xa, xb, ya, yb, za, zb, stage, newest, acc, table, mask, ids, sem, sems):
        def copy(x):
            return pltpu.make_async_copy(src.at[:, x], stage.at[x % slots], sem.at[x % slots])

        def at(cell):
            return newest[:, cell * LANES : (cell + 1) * LANES]

        small = [
            pltpu.make_async_copy(table_in, table, sems.at[0]),
            pltpu.make_async_copy(mask_in, mask, sems.at[1]),
            pltpu.make_async_copy(ids_in, ids, sems.at[2]),
        ]
        for item in small:
            item.start()
        for x in range(slots):
            copy(x).start()
        for item in small:
            item.wait()
        lane = lax.broadcasted_iota(jnp.int32, (columns, LANES), 1)
        one = lax.broadcasted_iota(jnp.int32, (1, LANES), 1)
        z_up = jnp.where(one == LANES - 1, 0.0, 1.0 + advection[2])
        z_down = jnp.where(one == 0, 0.0, 1.0 - advection[2])
        first = jnp.zeros((columns, LANES), F32)
        last = jnp.zeros((columns, LANES), F32)

        def apply(x, first, last):
            stand = ids[x]
            drag = jnp.zeros(stand.shape, F32)
            for s in range(stands):
                drag = jnp.where(stand == s, table[s] * mask[s].astype(F32), drag)
            for y in range(sy):
                cell = x * sy + y
                centre = at(cell)
                out = (6.0 + drag[y : y + 1, :]) * centre
                if x < sx - 1:
                    out = out - (1.0 + advection[0]) * at(cell + sy)
                if x > 0:
                    out = out - (1.0 - advection[0]) * at(cell - sy)
                if y < sy - 1:
                    out = out - (1.0 + advection[1]) * at(cell + 1)
                if y > 0:
                    out = out - (1.0 - advection[1]) * at(cell - 1)
                out = out - z_up * pltpu.roll(centre, LANES - 1, 1)
                out = out - z_down * pltpu.roll(centre, 1, 1)
                applied[:, cell * LANES : (cell + 1) * LANES] = out
                turned = pltpu.roll(centre, cell, 1) if cell else centre
                first = jnp.where(lane == cell, turned, first)
                last = jnp.where(lane == (cell - 1) % LANES, turned, last)
            return first, last

        for x in range(sx):
            copy(x).wait()
            for group in range(0, sy, 8):
                for base in range(0, rows, 32):
                    turned = pltpu.einshape("jyl->yjl", stage[x % slots, base : base + 32, group : group + 8, :])
                    for y in range(8):
                        cell = x * sy + group + y
                        cols = slice(cell * LANES, (cell + 1) * LANES)
                        high, low = split(turned[y])
                        halves[base : base + 32, cols] = high
                        halves[rows + base : rows + base + 32, cols] = low
                        if base >= rows - columns:
                            place = base - (rows - columns)
                            newest[place : place + 32, cols] = turned[y]
            if x + slots < sx:
                copy(x + slots).start()
            cols = slice(x * sy * LANES, (x + 1) * sy * LANES)
            gram = narrow(halves[:, cols], halves[0:rows, cols], ROW_DIMS)
            if x == 0:
                acc[...] = gram
            else:
                acc[...] += gram
            if x > 0:
                first, last = apply(x - 1, first, last)
        first, last = apply(sx - 1, first, last)
        even = even_here("gz", (columns, LANES))
        for y in range(sy):
            low, high = at(y), at((sx - 1) * sy + y)
            xa[y] = jnp.where(even, high, low)
            xb[y] = jnp.where(even, low, high)
        even = even_here("gx", (columns, LANES))
        for x in range(sx):
            low, high = at(x * sy), at(x * sy + sy - 1)
            ya[x] = jnp.where(even, high, low)
            yb[x] = jnp.where(even, low, high)
        even = even_here("gy", (columns, LANES))
        za[...] = jnp.where(even, last, first)
        zb[...] = jnp.where(even, first, last)
        cross = acc[rows : 2 * rows, :]
        own[...] = acc[0:rows, :] + cross + cross.T

    vmem = pl.BlockSpec(memory_space=pltpu.VMEM)
    return pl.pallas_call(
        kernel,
        in_specs=[pl.BlockSpec(memory_space=pltpu.HBM)] * 4,
        out_specs=[vmem] * 9,
        out_shape=[
            pltpu.VMEM((2 * rows, cells * LANES), BF16),
            pltpu.VMEM((columns, cells * LANES), F32),
            pltpu.VMEM((rows, rows), F32),
            pltpu.VMEM((sy, columns, LANES), F32),
            pltpu.VMEM((sy, columns, LANES), F32),
            pltpu.VMEM((sx, columns, LANES), F32),
            pltpu.VMEM((sx, columns, LANES), F32),
            pltpu.VMEM((columns, LANES), F32),
            pltpu.VMEM((columns, LANES), F32),
        ],
        scratch_shapes=[
            pltpu.VMEM((slots, rows, sy, LANES), F32),
            pltpu.VMEM((columns, cells * LANES), F32),
            pltpu.VMEM((2 * rows, rows), F32),
            pltpu.SMEM((stands,), F32),
            pltpu.SMEM((stands,), jnp.int32),
            pltpu.VMEM(stand_id.shape, jnp.int32),
            pltpu.SemaphoreType.DMA((slots,)),
            pltpu.SemaphoreType.DMA((3,)),
        ],
        compiler_params=pltpu.CompilerParams(vmem_limit_bytes=16 * 2**20),
        name="local_part",
    )(*[pltpu.with_memory_space_constraint(v, pltpu.HBM) for v in (drag_table, stand_mask, stand_id, basis)])


def products(halves, applied, own, halos, scale, sx, sy):
    rows2, width = halves.shape
    rows = rows2 // 2
    columns = applied.shape[0]
    half = rows // 2
    size = rows + half + columns + 16
    chunks = 4

    def kernel(halves, applied, own, xa, xb, ya, yb, za, zb, both, keep, give, passed, packed):
        def sides(axis, weight, one, two):
            index = lax.axis_index(axis)
            even = even_here(axis, (columns, LANES))
            down = jnp.where(index == 0, 0.0, 1.0 - weight)
            up = jnp.where(index == lax.axis_size(axis) - 1, 0.0, 1.0 + weight)
            low = [down * jnp.where(even, b, a) for a, b in zip(one, two)]
            high = [up * jnp.where(even, a, b) for a, b in zip(one, two)]
            return low, high

        lane = lax.broadcasted_iota(jnp.int32, (columns, LANES), 1)
        (z_low,), (z_high,) = sides("gy", advection[2], [za[...]], [zb[...]])
        cross, square = None, None
        for x in range(sx):
            if x == 0 or x == sx - 1:
                x_low, x_high = sides("gz", advection[0], [xa[y] for y in range(sy)], [xb[y] for y in range(sy)])
            (y_low,), (y_high,) = sides("gx", advection[1], [ya[x]], [yb[x]])
            for y in range(sy):
                cell = x * sy + y
                cols = slice(cell * LANES, (cell + 1) * LANES)
                value = applied[:, cols]
                if x == 0:
                    value = value - x_low[y]
                if x == sx - 1:
                    value = value - x_high[y]
                if y == 0:
                    value = value - y_low
                if y == sy - 1:
                    value = value - y_high
                shift = (1 - cell) % LANES
                low = pltpu.roll(z_low, shift, 1) if shift else z_low
                shift = (LANES - 1 - cell) % LANES
                high = pltpu.roll(z_high, shift, 1) if shift else z_high
                edge = jnp.where(lane == 0, low, jnp.where(lane == LANES - 1, high, 0.0))
                top, rest = split(value - edge)
                both[0:columns, cols] = top
                both[columns:, cols] = rest
            if (x + 1) % (sx // chunks) == 0:
                cols = slice((x + 1 - sx // chunks) * sy * LANES, (x + 1) * sy * LANES)
                one = narrow(halves[:, cols], both[:, cols], ROW_DIMS)
                two = narrow(both[:, cols], both[:, cols], ROW_DIMS)
                cross = one if cross is None else cross + one
                square = two if square is None else square + two
        mixed = cross[0:rows, :] + cross[rows:, :]
        coeffs = (mixed[:, 0:columns] + mixed[:, columns:]) * scale
        square = square[0:columns, :] + square[columns:, :]
        square = (square[:, 0:columns] + square[:, columns:]) * scale
        corner = own[half:, half:] * scale
        row = lax.broadcasted_iota(jnp.int32, (half, half), 0)
        col = lax.broadcasted_iota(jnp.int32, (half, half), 1)
        packed[0:half, :] = own[0:half, half:] * scale
        packed[half:rows, :] = jnp.where(row <= col, own[0:half, 0:half] * scale, corner)
        packed[rows : rows + half, 0:columns] = coeffs[0:half, :]
        packed[rows : rows + half, columns:] = coeffs[half:, :]
        packed[rows + half : rows + half + columns, :] = jnp.zeros((columns, LANES), F32)
        packed[rows + half : rows + half + columns, 0:columns] = square
        diag = jnp.sum(jnp.where(row == col, corner, 0.0), axis=0, keepdims=True)
        packed[rows + half + columns :, :] = jnp.broadcast_to(diag, (16, LANES))
        core = lax.axis_index("gz") % 2
        part = size // 2
        keep[...] = packed[pl.ds(pl.multiple_of(core * part, 8), part), :]
        give[...] = packed[pl.ds(pl.multiple_of((1 - core) * part, 8), part), :]

    vmem = pl.BlockSpec(memory_space=pltpu.VMEM)
    return pl.pallas_call(
        kernel,
        in_specs=[vmem] * 9,
        out_specs=[vmem] * 4,
        out_shape=[
            pltpu.VMEM((2 * columns, width), BF16),
            pltpu.VMEM((size // 2, LANES), F32),
            pltpu.VMEM((size // 2, LANES), F32),
            pltpu.VMEM((rows2, width), BF16),
        ],
        input_output_aliases={0: 3},
        scratch_shapes=[pltpu.VMEM((size, LANES), F32)],
        compiler_params=pltpu.CompilerParams(vmem_limit_bytes=8 * 2**20),
        name="products",
    )(halves, applied, own, *[resident(h) for h in halos])


def finish(part, other, halves, applied, sx, sy):
    rows = halves.shape[0] // 2
    columns = applied.shape[0] // 2
    half = rows // 2
    width = sy * LANES
    size = part.shape[0]

    def kernel(part, other, basis, block, fresh, coeffs_out, factor_out, staged, packed, residual, sem_out):
        core = lax.axis_index("gz") % 2
        packed[pl.ds(pl.multiple_of(core * size, 8), size), :] = part[...]
        packed[pl.ds(pl.multiple_of((1 - core) * size, 8), size), :] = other[...]
        row = lax.broadcasted_iota(jnp.int32, (half, half), 0)
        col = lax.broadcasted_iota(jnp.int32, (half, half), 1)
        mixed = packed[half:rows, :]
        upper = jnp.where(row < col, mixed, 0.0)
        s11 = upper + upper.T + jnp.where(row == col, mixed, 0.0)
        lower = jnp.where(row > col, mixed, 0.0)
        diag = packed[rows + half + columns : rows + half + columns + 1, :]
        s22 = lower + lower.T + jnp.where(row == col, diag, 0.0)
        s12 = packed[0:half, :]
        coeffs = jnp.concatenate(
            [packed[rows : rows + half, 0:columns], packed[rows : rows + half, columns:]], axis=0
        )
        coeffs_out[...] = coeffs
        turned = coeffs.T
        left, right = turned[:, 0:half], turned[:, half:]
        first = exact(left, s11) + exact(right, s12, ROW_DIMS) - 2.0 * left
        second = exact(left, s12) + exact(right, s22) - 2.0 * right
        gram = packed[rows + half : rows + half + columns, 0:columns]
        gram = gram + exact(first, left, ROW_DIMS) + exact(second, right, ROW_DIMS)
        gram = 0.5 * (gram + gram.T)
        eye = (
            lax.broadcasted_iota(jnp.int32, (columns, columns), 0)
            == lax.broadcasted_iota(jnp.int32, (columns, columns), 1)
        ).astype(F32)
        work = jnp.concatenate([gram, eye], axis=1)
        turned_both = jnp.concatenate(split(turned), axis=0)
        tiles = [work[t : t + 8, :] for t in range(0, columns, 8)]
        sub = lax.broadcasted_iota(jnp.int32, (8, LANES), 0)
        piece = sx * width // columns
        for j in range(columns):
            pivot_tile = tiles[j // 8]
            pivot = pivot_tile[j % 8 : j % 8 + 1, j : j + 1]
            scaled = pivot_tile[j % 8 : j % 8 + 1, :] * (1.0 / pivot)
            for t in range(j // 8, columns // 8):
                times = jnp.broadcast_to(tiles[t][:, j : j + 1], (8, LANES))
                if t == j // 8:
                    times = jnp.where(sub > j % 8, times, 0.0)
                tiles[t] = tiles[t] - times * scaled
            cols = slice(j * piece, (j + 1) * piece)
            big = narrow(turned_both, basis[0:rows, cols])
            taken = big[0:columns] + big[columns:] + narrow(turned_both[0:columns], basis[rows:, cols])
            value = (block[0:columns, cols].astype(F32) - taken) + block[columns:, cols].astype(F32)
            high, low = split(value)
            residual[0:columns, cols] = high
            residual[columns:, cols] = low
        solved = jnp.concatenate(tiles, axis=0)
        tri_row = lax.broadcasted_iota(jnp.int32, (columns, LANES), 0)
        tri_col = lax.broadcasted_iota(jnp.int32, (columns, LANES), 1)
        pivots = jnp.sum(jnp.where(tri_row == tri_col, solved, 0.0), axis=1, keepdims=True)
        inverse = lax.rsqrt(pivots)
        inverse = inverse * (1.5 - 0.5 * pivots * inverse * inverse)
        solved = solved * inverse
        factor_out[...] = jnp.where(tri_row <= tri_col, solved, 0.0)[:, 0:columns]
        inv_both = jnp.concatenate(split(solved[:, columns:]), axis=0)
        outs = []
        for x in range(sx):
            cols = slice(x * width, (x + 1) * width)
            big = narrow(inv_both, residual[0:columns, cols])
            value = big[0:columns] + big[columns:] + narrow(inv_both[0:columns], residual[columns:, cols])
            slot = x % 2
            if x >= 2:
                outs[x - 2].wait()
            for group in range(0, sy, 8):
                rows_y = [value[:, (group + y) * LANES : (group + y + 1) * LANES][None] for y in range(8)]
                staged[slot, :, group : group + 8, :] = pltpu.einshape("yjl->jyl", jnp.concatenate(rows_y, axis=0))
            outs.append(pltpu.make_async_copy(staged.at[slot], fresh.at[:, x], sem_out.at[slot]))
            outs[x].start()
        outs[sx - 2].wait()
        outs[sx - 1].wait()

    vmem = pl.BlockSpec(memory_space=pltpu.VMEM)
    anywhere = pl.BlockSpec(memory_space=pl.ANY)
    return pl.pallas_call(
        kernel,
        in_specs=[vmem] * 4,
        out_specs=[anywhere, vmem, vmem],
        out_shape=[
            jax.ShapeDtypeStruct((columns, sx, sy, LANES), F32),
            jax.ShapeDtypeStruct((rows, columns), F32),
            jax.ShapeDtypeStruct((columns, columns), F32),
        ],
        scratch_shapes=[
            pltpu.VMEM((2, columns, sy, LANES), F32),
            pltpu.VMEM((2 * size, LANES), F32),
            pltpu.VMEM(applied.shape, BF16),
            pltpu.SemaphoreType.DMA((2,)),
        ],
        compiler_params=pltpu.CompilerParams(vmem_limit_bytes=14 * 2**20),
        name="finish",
    )(resident(part), resident(other), halves, applied)


def swap(one, two, axis):
    count = lax.axis_size(axis)
    near = [(i, i ^ 1) for i in range(count)]
    far = [(i, (i - 1) % count if i % 2 == 0 else (i + 1) % count) for i in range(count)]
    return lax.ppermute(one, axis, near), lax.ppermute(two, axis, far)


def body(basis, stand_id, drag_table, stand_mask):
    blocks, columns, sx, sy, sz = basis.shape
    ncells = sx * sy * sz * lax.axis_size("gx") * lax.axis_size("gy") * lax.axis_size("gz")
    halves, applied, own, xa, xb, ya, yb, za, zb = local_part(
        basis.reshape(blocks * columns, sx, sy, sz), stand_id, drag_table, stand_mask
    )
    halos = (*swap(xa, xb, "gz"), *swap(ya, yb, "gx"), *swap(za, zb, "gy"))
    applied, keep, give, halves = products(halves, applied, own, halos, 1.0 / ncells, sx, sy)
    part, other = total(keep, give)
    fresh_block, coeffs, factor = finish(part, other, halves, applied, sx, sy)
    return fresh_block, coeffs.reshape(blocks, columns, columns), factor


def solution(mesh):
    placed = (P(None, None, "gz", "gx", "gy"), P("gz", "gx", "gy"), P(), P())
    return jax.shard_map(
        body,
        mesh=mesh,
        in_specs=placed,
        out_specs=(P(None, "gz", "gx", "gy"), P(), P()),
        check_vma=False,
    )
```

```python
import jax
import jax.numpy as jnp
from jax import lax
from jax.experimental import pallas as pl
from jax.experimental.pallas import tpu as pltpu
from jax.sharding import PartitionSpec as P

advection = (0.3, 0.2, 0.1)
ROW_DIMS = (((1,), (1,)), ((), ()))
MAT_DIMS = (((1,), (0,)), ((), ()))
LANES = 128
F32 = jnp.float32
BF16 = jnp.bfloat16


def exchange(value, axis, mask):
    pairs = [(source, source ^ mask) for source in range(lax.axis_size(axis))]
    return lax.ppermute(value, axis, pairs)


def quad_sum(value, axis, masks):
    parts = [exchange(value, axis, mask) for mask in masks]
    return (value + parts[0]) + (parts[1] + parts[2])


def total(keep, give):
    part = keep + exchange(give, "gz", 1)
    part = quad_sum(part, "gz", (2, 4, 6))
    part = quad_sum(part, "gy", (1, 2, 3))
    part = quad_sum(part, "gx", (1, 2, 3))
    return part, exchange(part, "gz", 1)


def exact(left, right, numbers=MAT_DIMS):
    return lax.dot_general(left, right, numbers, precision=lax.Precision.HIGHEST, preferred_element_type=F32)


def narrow(left, right, numbers=MAT_DIMS):
    return lax.dot_general(left, right, numbers, preferred_element_type=F32)


def split(value):
    high = value.astype(BF16)
    return high, (value - high.astype(F32)).astype(BF16)


def resident(value):
    return pltpu.with_memory_space_constraint(value, pltpu.VMEM)


def even_here(axis, shape):
    return jnp.full(shape, lax.axis_index(axis) % 2, jnp.int32) == 0


def local_part(basis, stand_id, drag_table, stand_mask):
    rows, sx, sy, _ = basis.shape
    columns = rows // 4
    cells = sx * sy
    stands = drag_table.shape[0]
    slots = 3

    def kernel(table_in, mask_in, ids_in, src, halves, applied, own, xa, xb, ya, yb, za, zb, stage, newest, acc, table, mask, ids, sem, sems):
        def copy(x):
            return pltpu.make_async_copy(src.at[:, x], stage.at[x % slots], sem.at[x % slots])

        def at(cell):
            return newest[:, cell * LANES : (cell + 1) * LANES]

        small = [
            pltpu.make_async_copy(table_in, table, sems.at[0]),
            pltpu.make_async_copy(mask_in, mask, sems.at[1]),
            pltpu.make_async_copy(ids_in, ids, sems.at[2]),
        ]
        for x in range(slots):
            copy(x).start()
        for item in small:
            item.start()
        lane = lax.broadcasted_iota(jnp.int32, (columns, LANES), 1)
        one = lax.broadcasted_iota(jnp.int32, (1, LANES), 1)
        z_up = jnp.where(one == LANES - 1, 0.0, 1.0 + advection[2])
        z_down = jnp.where(one == 0, 0.0, 1.0 - advection[2])
        first = jnp.zeros((columns, LANES), F32)
        last = jnp.zeros((columns, LANES), F32)

        def apply(x, first, last):
            stand = ids[x]
            drag = jnp.zeros(stand.shape, F32)
            for s in range(stands):
                drag = jnp.where(stand == s, table[s] * mask[s].astype(F32), drag)
            for y in range(sy):
                cell = x * sy + y
                centre = at(cell)
                out = (6.0 + drag[y : y + 1, :]) * centre
                if x < sx - 1:
                    out = out - (1.0 + advection[0]) * at(cell + sy)
                if x > 0:
                    out = out - (1.0 - advection[0]) * at(cell - sy)
                if y < sy - 1:
                    out = out - (1.0 + advection[1]) * at(cell + 1)
                if y > 0:
                    out = out - (1.0 - advection[1]) * at(cell - 1)
                out = out - z_up * pltpu.roll(centre, LANES - 1, 1)
                out = out - z_down * pltpu.roll(centre, 1, 1)
                applied[:, cell * LANES : (cell + 1) * LANES] = out
                turned = pltpu.roll(centre, cell, 1) if cell else centre
                first = jnp.where(lane == cell, turned, first)
                last = jnp.where(lane == (cell - 1) % LANES, turned, last)
            return first, last

        for x in range(sx):
            copy(x).wait()
            for group in range(0, sy, 8):
                for base in range(0, rows, 32):
                    turned = pltpu.einshape("jyl->yjl", stage[x % slots, base : base + 32, group : group + 8, :])
                    for y in range(8):
                        cell = x * sy + group + y
                        cols = slice(cell * LANES, (cell + 1) * LANES)
                        high, low = split(turned[y])
                        halves[base : base + 32, cols] = high
                        halves[rows + base : rows + base + 32, cols] = low
                        if base >= rows - columns:
                            place = base - (rows - columns)
                            newest[place : place + 32, cols] = turned[y]
            if x + slots < sx:
                copy(x + slots).start()
            cols = slice(x * sy * LANES, (x + 1) * sy * LANES)
            gram = narrow(halves[:, cols], halves[0:rows, cols], ROW_DIMS)
            if x == 0:
                acc[...] = gram
            else:
                acc[...] += gram
            if x == 0:
                for item in small:
                    item.wait()
            if x > 0:
                first, last = apply(x - 1, first, last)
        first, last = apply(sx - 1, first, last)
        even = even_here("gz", (columns, LANES))
        for y in range(sy):
            low, high = at(y), at((sx - 1) * sy + y)
            xa[y] = jnp.where(even, high, low)
            xb[y] = jnp.where(even, low, high)
        even = even_here("gx", (columns, LANES))
        for x in range(sx):
            low, high = at(x * sy), at(x * sy + sy - 1)
            ya[x] = jnp.where(even, high, low)
            yb[x] = jnp.where(even, low, high)
        even = even_here("gy", (columns, LANES))
        za[...] = jnp.where(even, last, first)
        zb[...] = jnp.where(even, first, last)
        cross = acc[rows : 2 * rows, :]
        own[...] = acc[0:rows, :] + cross + cross.T

    vmem = pl.BlockSpec(memory_space=pltpu.VMEM)
    return pl.pallas_call(
        kernel,
        in_specs=[pl.BlockSpec(memory_space=pltpu.HBM)] * 4,
        out_specs=[vmem] * 9,
        out_shape=[
            pltpu.VMEM((2 * rows, cells * LANES), BF16),
            pltpu.VMEM((columns, cells * LANES), F32),
            pltpu.VMEM((rows, rows), F32),
            pltpu.VMEM((sy, columns, LANES), F32),
            pltpu.VMEM((sy, columns, LANES), F32),
            pltpu.VMEM((sx, columns, LANES), F32),
            pltpu.VMEM((sx, columns, LANES), F32),
            pltpu.VMEM((columns, LANES), F32),
            pltpu.VMEM((columns, LANES), F32),
        ],
        scratch_shapes=[
            pltpu.VMEM((slots, rows, sy, LANES), F32),
            pltpu.VMEM((columns, cells * LANES), F32),
            pltpu.VMEM((2 * rows, rows), F32),
            pltpu.SMEM((stands,), F32),
            pltpu.SMEM((stands,), jnp.int32),
            pltpu.VMEM(stand_id.shape, jnp.int32),
            pltpu.SemaphoreType.DMA((slots,)),
            pltpu.SemaphoreType.DMA((3,)),
        ],
        compiler_params=pltpu.CompilerParams(vmem_limit_bytes=16 * 2**20),
        name="local_part",
    )(*[pltpu.with_memory_space_constraint(v, pltpu.HBM) for v in (drag_table, stand_mask, stand_id, basis)])


def products(halves, applied, own, halos, scale, sx, sy):
    rows2, width = halves.shape
    rows = rows2 // 2
    columns = applied.shape[0]
    half = rows // 2
    size = rows + half + columns // 2 + 16
    chunks = 4

    def kernel(halves, applied, own, xa, xb, ya, yb, za, zb, both, keep, give, passed, packed):
        def sides(axis, weight, one, two):
            index = lax.axis_index(axis)
            even = even_here(axis, (columns, LANES))
            down = jnp.where(index == 0, 0.0, 1.0 - weight)
            up = jnp.where(index == lax.axis_size(axis) - 1, 0.0, 1.0 + weight)
            low = [down * jnp.where(even, b, a) for a, b in zip(one, two)]
            high = [up * jnp.where(even, a, b) for a, b in zip(one, two)]
            return low, high

        lane = lax.broadcasted_iota(jnp.int32, (columns, LANES), 1)
        (z_low,), (z_high,) = sides("gy", advection[2], [za[...]], [zb[...]])
        cross, square = None, None
        for x in range(sx):
            if x == 0 or x == sx - 1:
                x_low, x_high = sides("gz", advection[0], [xa[y] for y in range(sy)], [xb[y] for y in range(sy)])
            (y_low,), (y_high,) = sides("gx", advection[1], [ya[x]], [yb[x]])
            for y in range(sy):
                cell = x * sy + y
                cols = slice(cell * LANES, (cell + 1) * LANES)
                value = applied[:, cols]
                if x == 0:
                    value = value - x_low[y]
                if x == sx - 1:
                    value = value - x_high[y]
                if y == 0:
                    value = value - y_low
                if y == sy - 1:
                    value = value - y_high
                shift = (1 - cell) % LANES
                low = pltpu.roll(z_low, shift, 1) if shift else z_low
                shift = (LANES - 1 - cell) % LANES
                high = pltpu.roll(z_high, shift, 1) if shift else z_high
                edge = jnp.where(lane == 0, low, jnp.where(lane == LANES - 1, high, 0.0))
                top, rest = split(value - edge)
                both[0:columns, cols] = top
                both[columns:, cols] = rest
            if (x + 1) % (sx // chunks) == 0:
                cols = slice((x + 1 - sx // chunks) * sy * LANES, (x + 1) * sy * LANES)
                one = narrow(both[:, cols], halves[:, cols], ROW_DIMS)
                two = narrow(both[:, cols], both[:, cols], ROW_DIMS)
                cross = one if cross is None else cross + one
                square = two if square is None else square + two
        mixed = cross[:, 0:rows] + cross[:, rows:]
        turned = (mixed[0:columns, :] + mixed[columns:, :]) * scale
        square = square[0:columns, :] + square[columns:, :]
        square = (square[:, 0:columns] + square[:, columns:]) * scale
        corner = own[half:, half:] * scale
        row = lax.broadcasted_iota(jnp.int32, (half, half), 0)
        col = lax.broadcasted_iota(jnp.int32, (half, half), 1)
        packed[0:half, :] = own[0:half, half:] * scale
        packed[half:rows, :] = jnp.where(row <= col, own[0:half, 0:half] * scale, corner)
        packed[rows : rows + columns, :] = turned[:, 0:half]
        packed[rows + columns : rows + half, :] = turned[:, half:]
        tail = rows + half + columns // 2
        packed[rows + half : tail, 0:columns] = square[0 : columns // 2, :]
        packed[rows + half : tail, columns:] = square[columns // 2 :, :]
        diag = jnp.sum(jnp.where(row == col, corner, 0.0), axis=0, keepdims=True)
        packed[tail:, :] = jnp.broadcast_to(diag, (16, LANES))
        core = lax.axis_index("gz") % 2
        part = size // 2
        keep[...] = packed[pl.ds(pl.multiple_of(core * part, 8), part), :]
        give[...] = packed[pl.ds(pl.multiple_of((1 - core) * part, 8), part), :]

    vmem = pl.BlockSpec(memory_space=pltpu.VMEM)
    return pl.pallas_call(
        kernel,
        in_specs=[vmem] * 9,
        out_specs=[vmem] * 4,
        out_shape=[
            pltpu.VMEM((2 * columns, width), BF16),
            pltpu.VMEM((size // 2, LANES), F32),
            pltpu.VMEM((size // 2, LANES), F32),
            pltpu.VMEM((rows2, width), BF16),
        ],
        input_output_aliases={0: 3},
        scratch_shapes=[pltpu.VMEM((size, LANES), F32)],
        compiler_params=pltpu.CompilerParams(vmem_limit_bytes=8 * 2**20),
        name="products",
    )(halves, applied, own, *[resident(h) for h in halos])


def finish(part, other, halves, applied, sx, sy):
    rows = halves.shape[0] // 2
    columns = applied.shape[0] // 2
    half = rows // 2
    width = sy * LANES
    size = part.shape[0]

    def kernel(part, other, basis, block, fresh, coeffs_out, factor_out, staged, packed, residual, sem_out):
        core = lax.axis_index("gz") % 2
        packed[pl.ds(pl.multiple_of(core * size, 8), size), :] = part[...]
        packed[pl.ds(pl.multiple_of((1 - core) * size, 8), size), :] = other[...]
        row = lax.broadcasted_iota(jnp.int32, (half, half), 0)
        col = lax.broadcasted_iota(jnp.int32, (half, half), 1)
        mixed = packed[half:rows, :]
        upper = jnp.where(row < col, mixed, 0.0)
        s11 = upper + upper.T + jnp.where(row == col, mixed, 0.0)
        lower = jnp.where(row > col, mixed, 0.0)
        tail = rows + half + columns // 2
        diag = packed[tail : tail + 1, :]
        s22 = lower + lower.T + jnp.where(row == col, diag, 0.0)
        s12 = packed[0:half, :]
        left, right = packed[rows : rows + columns, :], packed[rows + columns : rows + half, :]
        turned = jnp.concatenate([left, right], axis=1)
        coeffs_out[...] = turned.T
        first = exact(left, s11) + exact(right, s12, ROW_DIMS) - 2.0 * left
        second = exact(left, s12) + exact(right, s22) - 2.0 * right
        gram = jnp.concatenate([packed[rows + half : tail, 0:columns], packed[rows + half : tail, columns:]], axis=0)
        gram = gram + exact(first, left, ROW_DIMS) + exact(second, right, ROW_DIMS)
        gram = 0.5 * (gram + gram.T)
        eye = (
            lax.broadcasted_iota(jnp.int32, (columns, columns), 0)
            == lax.broadcasted_iota(jnp.int32, (columns, columns), 1)
        ).astype(F32)
        work = jnp.concatenate([gram, eye], axis=1)
        turned_both = jnp.concatenate(split(turned), axis=0)
        tiles = [work[t : t + 8, :] for t in range(0, columns, 8)]
        sub = lax.broadcasted_iota(jnp.int32, (8, LANES), 0)
        piece = sx * width // columns
        for j in range(columns):
            pivot_tile = tiles[j // 8]
            pivot = pivot_tile[j % 8 : j % 8 + 1, j : j + 1]
            scaled = pivot_tile[j % 8 : j % 8 + 1, :] * (1.0 / pivot)
            for t in range(j // 8, columns // 8):
                times = jnp.broadcast_to(tiles[t][:, j : j + 1], (8, LANES))
                if t == j // 8:
                    times = jnp.where(sub > j % 8, times, 0.0)
                tiles[t] = tiles[t] - times * scaled
            cols = slice(j * piece, (j + 1) * piece)
            big = narrow(turned_both, basis[0:rows, cols])
            taken = big[0:columns] + big[columns:] + narrow(turned_both[0:columns], basis[rows:, cols])
            value = (block[0:columns, cols].astype(F32) - taken) + block[columns:, cols].astype(F32)
            high, low = split(value)
            residual[0:columns, cols] = high
            residual[columns:, cols] = low
        solved = jnp.concatenate(tiles, axis=0)
        tri_row = lax.broadcasted_iota(jnp.int32, (columns, LANES), 0)
        tri_col = lax.broadcasted_iota(jnp.int32, (columns, LANES), 1)
        pivots = jnp.sum(jnp.where(tri_row == tri_col, solved, 0.0), axis=1, keepdims=True)
        inverse = lax.rsqrt(pivots)
        inverse = inverse * (1.5 - 0.5 * pivots * inverse * inverse)
        solved = solved * inverse
        factor_out[...] = jnp.where(tri_row <= tri_col, solved, 0.0)[:, 0:columns]
        inv_both = jnp.concatenate(split(solved[:, columns:]), axis=0)
        outs = []
        for x in range(sx):
            cols = slice(x * width, (x + 1) * width)
            big = narrow(inv_both, residual[0:columns, cols])
            value = big[0:columns] + big[columns:] + narrow(inv_both[0:columns], residual[columns:, cols])
            slot = x % 2
            if x >= 2:
                outs[x - 2].wait()
            for group in range(0, sy, 8):
                rows_y = [value[:, (group + y) * LANES : (group + y + 1) * LANES][None] for y in range(8)]
                staged[slot, :, group : group + 8, :] = pltpu.einshape("yjl->jyl", jnp.concatenate(rows_y, axis=0))
            outs.append(pltpu.make_async_copy(staged.at[slot], fresh.at[:, x], sem_out.at[slot]))
            outs[x].start()
        outs[sx - 2].wait()
        outs[sx - 1].wait()

    vmem = pl.BlockSpec(memory_space=pltpu.VMEM)
    anywhere = pl.BlockSpec(memory_space=pl.ANY)
    return pl.pallas_call(
        kernel,
        in_specs=[vmem] * 4,
        out_specs=[anywhere, vmem, vmem],
        out_shape=[
            jax.ShapeDtypeStruct((columns, sx, sy, LANES), F32),
            jax.ShapeDtypeStruct((rows, columns), F32),
            jax.ShapeDtypeStruct((columns, columns), F32),
        ],
        scratch_shapes=[
            pltpu.VMEM((2, columns, sy, LANES), F32),
            pltpu.VMEM((2 * size, LANES), F32),
            pltpu.VMEM(applied.shape, BF16),
            pltpu.SemaphoreType.DMA((2,)),
        ],
        compiler_params=pltpu.CompilerParams(vmem_limit_bytes=14 * 2**20),
        name="finish",
    )(resident(part), resident(other), halves, applied)


def swap(one, two, axis):
    count = lax.axis_size(axis)
    near = [(i, i ^ 1) for i in range(count)]
    far = [(i, (i - 1) % count if i % 2 == 0 else (i + 1) % count) for i in range(count)]
    return lax.ppermute(one, axis, near), lax.ppermute(two, axis, far)


def body(basis, stand_id, drag_table, stand_mask):
    blocks, columns, sx, sy, sz = basis.shape
    ncells = sx * sy * sz * lax.axis_size("gx") * lax.axis_size("gy") * lax.axis_size("gz")
    halves, applied, own, xa, xb, ya, yb, za, zb = local_part(
        basis.reshape(blocks * columns, sx, sy, sz), stand_id, drag_table, stand_mask
    )
    halos = (*swap(xa, xb, "gz"), *swap(ya, yb, "gx"), *swap(za, zb, "gy"))
    applied, keep, give, halves = products(halves, applied, own, halos, 1.0 / ncells, sx, sy)
    part, other = total(keep, give)
    fresh_block, coeffs, factor = finish(part, other, halves, applied, sx, sy)
    return fresh_block, coeffs.reshape(blocks, columns, columns), factor


def solution(mesh):
    placed = (P(None, None, "gz", "gx", "gy"), P("gz", "gx", "gy"), P(), P())
    return jax.shard_map(
        body,
        mesh=mesh,
        in_specs=placed,
        out_specs=(P(None, "gz", "gx", "gy"), P(), P()),
        check_vma=False,
    )
```

```python
import jax
import jax.numpy as jnp
from jax import lax
from jax.experimental import pallas as pl
from jax.experimental.pallas import tpu as pltpu
from jax.sharding import PartitionSpec as P

advection = (0.3, 0.2, 0.1)
ROW_DIMS = (((1,), (1,)), ((), ()))
MAT_DIMS = (((1,), (0,)), ((), ()))
LANES = 128
F32 = jnp.float32
BF16 = jnp.bfloat16


def exchange(value, axis, mask):
    pairs = [(source, source ^ mask) for source in range(lax.axis_size(axis))]
    return lax.ppermute(value, axis, pairs)


def quad_sum(value, axis, masks):
    parts = [exchange(value, axis, mask) for mask in masks]
    return (value + parts[0]) + (parts[1] + parts[2])


def total(keep, give):
    part = keep + exchange(give, "gz", 1)
    part = quad_sum(part, "gz", (2, 4, 6))
    part = quad_sum(part, "gy", (1, 2, 3))
    part = quad_sum(part, "gx", (1, 2, 3))
    return part, exchange(part, "gz", 1)


def exact(left, right, numbers=MAT_DIMS):
    return lax.dot_general(left, right, numbers, precision=lax.Precision.HIGHEST, preferred_element_type=F32)


def narrow(left, right, numbers=MAT_DIMS):
    return lax.dot_general(left, right, numbers, preferred_element_type=F32)


def split(value):
    high = value.astype(BF16)
    return high, (value - high.astype(F32)).astype(BF16)


def resident(value):
    return pltpu.with_memory_space_constraint(value, pltpu.VMEM)


def even_here(axis, shape):
    return jnp.full(shape, lax.axis_index(axis) % 2, jnp.int32) == 0


def local_part(basis, stand_id, drag_table, stand_mask):
    rows, sx, sy, _ = basis.shape
    columns = rows // 4
    cells = sx * sy
    stands = drag_table.shape[0]
    slots = 3

    def kernel(table_in, mask_in, ids_in, src, halves, applied, own, xa, xb, ya, yb, za, zb, stage, newest, acc, table, mask, ids, sem, sems):
        def copy(x):
            return pltpu.make_async_copy(src.at[:, x], stage.at[x % slots], sem.at[x % slots])

        def at(cell):
            return newest[:, cell * LANES : (cell + 1) * LANES]

        small = [
            pltpu.make_async_copy(table_in, table, sems.at[0]),
            pltpu.make_async_copy(mask_in, mask, sems.at[1]),
            pltpu.make_async_copy(ids_in, ids, sems.at[2]),
        ]
        for x in range(slots):
            copy(x).start()
        for item in small:
            item.start()
        lane = lax.broadcasted_iota(jnp.int32, (columns, LANES), 1)
        one = lax.broadcasted_iota(jnp.int32, (1, LANES), 1)
        z_up = jnp.where(one == LANES - 1, 0.0, 1.0 + advection[2])
        z_down = jnp.where(one == 0, 0.0, 1.0 - advection[2])
        first = jnp.zeros((columns, LANES), F32)
        last = jnp.zeros((columns, LANES), F32)

        def apply(x, first, last):
            stand = ids[x]
            drag = jnp.zeros(stand.shape, F32)
            for s in range(stands):
                drag = jnp.where(stand == s, table[s] * mask[s].astype(F32), drag)
            for y in range(sy):
                cell = x * sy + y
                centre = at(cell)
                out = (6.0 + drag[y : y + 1, :]) * centre
                if x < sx - 1:
                    out = out - (1.0 + advection[0]) * at(cell + sy)
                if x > 0:
                    out = out - (1.0 - advection[0]) * at(cell - sy)
                if y < sy - 1:
                    out = out - (1.0 + advection[1]) * at(cell + 1)
                if y > 0:
                    out = out - (1.0 - advection[1]) * at(cell - 1)
                out = out - z_up * pltpu.roll(centre, LANES - 1, 1)
                out = out - z_down * pltpu.roll(centre, 1, 1)
                applied[:, cell * LANES : (cell + 1) * LANES] = out
                turned = pltpu.roll(centre, cell, 1) if cell else centre
                first = jnp.where(lane == cell, turned, first)
                last = jnp.where(lane == (cell - 1) % LANES, turned, last)
            return first, last

        for x in range(sx):
            copy(x).wait()
            for group in range(0, sy, 8):
                for base in range(0, rows, 32):
                    turned = pltpu.einshape("jyl->yjl", stage[x % slots, base : base + 32, group : group + 8, :])
                    for y in range(8):
                        cell = x * sy + group + y
                        cols = slice(cell * LANES, (cell + 1) * LANES)
                        high, low = split(turned[y])
                        halves[base : base + 32, cols] = high
                        halves[rows + base : rows + base + 32, cols] = low
                        if base >= rows - columns:
                            place = base - (rows - columns)
                            newest[place : place + 32, cols] = turned[y]
            if x + slots < sx:
                copy(x + slots).start()
            cols = slice(x * sy * LANES, (x + 1) * sy * LANES)
            gram = narrow(halves[:, cols], halves[0:rows, cols], ROW_DIMS)
            if x == 0:
                acc[...] = gram
            else:
                acc[...] += gram
            if x == 0:
                for item in small:
                    item.wait()
            if x > 0:
                first, last = apply(x - 1, first, last)
        first, last = apply(sx - 1, first, last)
        even = even_here("gz", (columns, LANES))
        for y in range(sy):
            low, high = at(y), at((sx - 1) * sy + y)
            xa[y] = jnp.where(even, high, low)
            xb[y] = jnp.where(even, low, high)
        even = even_here("gx", (columns, LANES))
        for x in range(sx):
            low, high = at(x * sy), at(x * sy + sy - 1)
            ya[x] = jnp.where(even, high, low)
            yb[x] = jnp.where(even, low, high)
        even = even_here("gy", (columns, LANES))
        za[...] = jnp.where(even, last, first)
        zb[...] = jnp.where(even, first, last)
        cross = acc[rows : 2 * rows, :]
        own[...] = acc[0:rows, :] + cross + cross.T

    vmem = pl.BlockSpec(memory_space=pltpu.VMEM)
    return pl.pallas_call(
        kernel,
        in_specs=[pl.BlockSpec(memory_space=pltpu.HBM)] * 4,
        out_specs=[vmem] * 9,
        out_shape=[
            pltpu.VMEM((2 * rows, cells * LANES), BF16),
            pltpu.VMEM((columns, cells * LANES), F32),
            pltpu.VMEM((rows, rows), F32),
            pltpu.VMEM((sy, columns, LANES), F32),
            pltpu.VMEM((sy, columns, LANES), F32),
            pltpu.VMEM((sx, columns, LANES), F32),
            pltpu.VMEM((sx, columns, LANES), F32),
            pltpu.VMEM((columns, LANES), F32),
            pltpu.VMEM((columns, LANES), F32),
        ],
        scratch_shapes=[
            pltpu.VMEM((slots, rows, sy, LANES), F32),
            pltpu.VMEM((columns, cells * LANES), F32),
            pltpu.VMEM((2 * rows, rows), F32),
            pltpu.SMEM((stands,), F32),
            pltpu.SMEM((stands,), jnp.int32),
            pltpu.VMEM(stand_id.shape, jnp.int32),
            pltpu.SemaphoreType.DMA((slots,)),
            pltpu.SemaphoreType.DMA((3,)),
        ],
        compiler_params=pltpu.CompilerParams(vmem_limit_bytes=16 * 2**20),
        name="local_part",
    )(*[pltpu.with_memory_space_constraint(v, pltpu.HBM) for v in (drag_table, stand_mask, stand_id, basis)])


def products(halves, applied, own, halos, scale, sx, sy):
    rows2, width = halves.shape
    rows = rows2 // 2
    columns = applied.shape[0]
    half = rows // 2
    size = rows + half + columns // 2 + 16
    chunks = 4

    def kernel(halves, applied, own, xa, xb, ya, yb, za, zb, both, keep, give, passed, packed):
        def sides(axis, weight, one, two):
            index = lax.axis_index(axis)
            even = even_here(axis, (columns, LANES))
            down = jnp.where(index == 0, 0.0, 1.0 - weight)
            up = jnp.where(index == lax.axis_size(axis) - 1, 0.0, 1.0 + weight)
            low = [down * jnp.where(even, b, a) for a, b in zip(one, two)]
            high = [up * jnp.where(even, a, b) for a, b in zip(one, two)]
            return low, high

        lane = lax.broadcasted_iota(jnp.int32, (columns, LANES), 1)
        (z_low,), (z_high,) = sides("gy", advection[2], [za[...]], [zb[...]])
        cross, square = None, None
        for x in range(sx):
            if x == 0 or x == sx - 1:
                x_low, x_high = sides("gz", advection[0], [xa[y] for y in range(sy)], [xb[y] for y in range(sy)])
            (y_low,), (y_high,) = sides("gx", advection[1], [ya[x]], [yb[x]])
            for y in range(sy):
                cell = x * sy + y
                cols = slice(cell * LANES, (cell + 1) * LANES)
                value = applied[:, cols]
                if x == 0:
                    value = value - x_low[y]
                if x == sx - 1:
                    value = value - x_high[y]
                if y == 0:
                    value = value - y_low
                if y == sy - 1:
                    value = value - y_high
                shift = (1 - cell) % LANES
                low = pltpu.roll(z_low, shift, 1) if shift else z_low
                shift = (LANES - 1 - cell) % LANES
                high = pltpu.roll(z_high, shift, 1) if shift else z_high
                edge = jnp.where(lane == 0, low, jnp.where(lane == LANES - 1, high, 0.0))
                top, rest = split(value - edge)
                both[0:columns, cols] = top
                both[columns:, cols] = rest
            if (x + 1) % (sx // chunks) == 0:
                cols = slice((x + 1 - sx // chunks) * sy * LANES, (x + 1) * sy * LANES)
                one = narrow(both[:, cols], halves[:, cols], ROW_DIMS)
                two = narrow(both[:, cols], both[:, cols], ROW_DIMS)
                cross = one if cross is None else cross + one
                square = two if square is None else square + two
        mixed = cross[:, 0:rows] + cross[:, rows:]
        turned = (mixed[0:columns, :] + mixed[columns:, :]) * scale
        square = square[0:columns, :] + square[columns:, :]
        square = (square[:, 0:columns] + square[:, columns:]) * scale
        corner = own[half:, half:] * scale
        row = lax.broadcasted_iota(jnp.int32, (half, half), 0)
        col = lax.broadcasted_iota(jnp.int32, (half, half), 1)
        packed[0:half, :] = own[0:half, half:] * scale
        packed[half:rows, :] = jnp.where(row <= col, own[0:half, 0:half] * scale, corner)
        packed[rows : rows + columns, :] = turned[:, 0:half]
        packed[rows + columns : rows + half, :] = turned[:, half:]
        tail = rows + half + columns // 2
        packed[rows + half : tail, 0:columns] = square[0 : columns // 2, :]
        packed[rows + half : tail, columns:] = square[columns // 2 :, :]
        diag = jnp.sum(jnp.where(row == col, corner, 0.0), axis=0, keepdims=True)
        packed[tail:, :] = jnp.broadcast_to(diag, (16, LANES))
        core = lax.axis_index("gz") % 2
        part = size // 2
        keep[...] = packed[pl.ds(pl.multiple_of(core * part, 8), part), :]
        give[...] = packed[pl.ds(pl.multiple_of((1 - core) * part, 8), part), :]

    vmem = pl.BlockSpec(memory_space=pltpu.VMEM)
    return pl.pallas_call(
        kernel,
        in_specs=[vmem] * 9,
        out_specs=[vmem] * 4,
        out_shape=[
            pltpu.VMEM((2 * columns, width), BF16),
            pltpu.VMEM((size // 2, LANES), F32),
            pltpu.VMEM((size // 2, LANES), F32),
            pltpu.VMEM((rows2, width), BF16),
        ],
        input_output_aliases={0: 3},
        scratch_shapes=[pltpu.VMEM((size, LANES), F32)],
        compiler_params=pltpu.CompilerParams(vmem_limit_bytes=8 * 2**20),
        name="products",
    )(halves, applied, own, *[resident(h) for h in halos])


def finish(part, other, halves, applied, sx, sy):
    rows = halves.shape[0] // 2
    columns = applied.shape[0] // 2
    half = rows // 2
    width = sy * LANES
    size = part.shape[0]
    depth = 4

    def kernel(part, other, basis, block, fresh, coeffs_out, factor_out, staged, packed, residual, sem_out):
        core = lax.axis_index("gz") % 2
        packed[pl.ds(pl.multiple_of(core * size, 8), size), :] = part[...]
        packed[pl.ds(pl.multiple_of((1 - core) * size, 8), size), :] = other[...]
        row = lax.broadcasted_iota(jnp.int32, (half, half), 0)
        col = lax.broadcasted_iota(jnp.int32, (half, half), 1)
        mixed = packed[half:rows, :]
        upper = jnp.where(row < col, mixed, 0.0)
        s11 = upper + upper.T + jnp.where(row == col, mixed, 0.0)
        lower = jnp.where(row > col, mixed, 0.0)
        tail = rows + half + columns // 2
        diag = packed[tail : tail + 1, :]
        s22 = lower + lower.T + jnp.where(row == col, diag, 0.0)
        s12 = packed[0:half, :]
        left, right = packed[rows : rows + columns, :], packed[rows + columns : rows + half, :]
        turned = jnp.concatenate([left, right], axis=1)
        coeffs_out[...] = turned.T
        square = jnp.concatenate(
            [jnp.concatenate([s11, s12], axis=1), jnp.concatenate([s12.T, s22], axis=1)], axis=0
        )
        middle = exact(turned, square) - 2.0 * turned
        gram = jnp.concatenate([packed[rows + half : tail, 0:columns], packed[rows + half : tail, columns:]], axis=0)
        gram = gram + exact(middle, turned, ROW_DIMS)
        gram = 0.5 * (gram + gram.T)
        eye = (
            lax.broadcasted_iota(jnp.int32, (columns, columns), 0)
            == lax.broadcasted_iota(jnp.int32, (columns, columns), 1)
        ).astype(F32)
        work = jnp.concatenate([gram, eye], axis=1)
        turned_both = jnp.concatenate(split(turned), axis=0)
        tiles = [work[t : t + 8, :] for t in range(0, columns, 8)]
        sub = lax.broadcasted_iota(jnp.int32, (8, LANES), 0)
        piece = sx * width // columns
        for j in range(columns):
            pivot_tile = tiles[j // 8]
            pivot = pivot_tile[j % 8 : j % 8 + 1, j : j + 1]
            scaled = pivot_tile[j % 8 : j % 8 + 1, :] * (1.0 / pivot)
            for t in range(j // 8, columns // 8):
                times = jnp.broadcast_to(tiles[t][:, j : j + 1], (8, LANES))
                if t == j // 8:
                    times = jnp.where(sub > j % 8, times, 0.0)
                tiles[t] = tiles[t] - times * scaled
            cols = slice(j * piece, (j + 1) * piece)
            big = narrow(turned_both, basis[0:rows, cols])
            taken = big[0:columns] + big[columns:] + narrow(turned_both[0:columns], basis[rows:, cols])
            value = (block[0:columns, cols].astype(F32) - taken) + block[columns:, cols].astype(F32)
            high, low = split(value)
            residual[0:columns, cols] = high
            residual[columns:, cols] = low
        solved = jnp.concatenate(tiles, axis=0)
        tri_row = lax.broadcasted_iota(jnp.int32, (columns, LANES), 0)
        tri_col = lax.broadcasted_iota(jnp.int32, (columns, LANES), 1)
        pivots = jnp.sum(jnp.where(tri_row == tri_col, solved, 0.0), axis=1, keepdims=True)
        inverse = lax.rsqrt(pivots)
        inverse = inverse * (1.5 - 0.5 * pivots * inverse * inverse)
        solved = solved * inverse
        factor_out[...] = jnp.where(tri_row <= tri_col, solved, 0.0)[:, 0:columns]
        inv_both = jnp.concatenate(split(solved[:, columns:]), axis=0)
        outs = []
        for x in range(sx):
            cols = slice(x * width, (x + 1) * width)
            big = narrow(inv_both, residual[0:columns, cols])
            value = big[0:columns] + big[columns:] + narrow(inv_both[0:columns], residual[columns:, cols])
            slot = x % depth
            if x >= depth:
                outs[x - depth].wait()
            for group in range(0, sy, 8):
                rows_y = [value[:, (group + y) * LANES : (group + y + 1) * LANES][None] for y in range(8)]
                staged[slot, :, group : group + 8, :] = pltpu.einshape("yjl->jyl", jnp.concatenate(rows_y, axis=0))
            outs.append(pltpu.make_async_copy(staged.at[slot], fresh.at[:, x], sem_out.at[slot]))
            outs[x].start()
        for x in range(sx - depth, sx):
            outs[x].wait()

    vmem = pl.BlockSpec(memory_space=pltpu.VMEM)
    anywhere = pl.BlockSpec(memory_space=pl.ANY)
    return pl.pallas_call(
        kernel,
        in_specs=[vmem] * 4,
        out_specs=[anywhere, vmem, vmem],
        out_shape=[
            jax.ShapeDtypeStruct((columns, sx, sy, LANES), F32),
            jax.ShapeDtypeStruct((rows, columns), F32),
            jax.ShapeDtypeStruct((columns, columns), F32),
        ],
        scratch_shapes=[
            pltpu.VMEM((depth, columns, sy, LANES), F32),
            pltpu.VMEM((2 * size, LANES), F32),
            pltpu.VMEM(applied.shape, BF16),
            pltpu.SemaphoreType.DMA((depth,)),
        ],
        compiler_params=pltpu.CompilerParams(vmem_limit_bytes=14 * 2**20),
        name="finish",
    )(resident(part), resident(other), halves, applied)


def swap(one, two, axis):
    count = lax.axis_size(axis)
    near = [(i, i ^ 1) for i in range(count)]
    far = [(i, (i - 1) % count if i % 2 == 0 else (i + 1) % count) for i in range(count)]
    return lax.ppermute(one, axis, near), lax.ppermute(two, axis, far)


def body(basis, stand_id, drag_table, stand_mask):
    blocks, columns, sx, sy, sz = basis.shape
    ncells = sx * sy * sz * lax.axis_size("gx") * lax.axis_size("gy") * lax.axis_size("gz")
    halves, applied, own, xa, xb, ya, yb, za, zb = local_part(
        basis.reshape(blocks * columns, sx, sy, sz), stand_id, drag_table, stand_mask
    )
    halos = (*swap(xa, xb, "gz"), *swap(ya, yb, "gx"), *swap(za, zb, "gy"))
    applied, keep, give, halves = products(halves, applied, own, halos, 1.0 / ncells, sx, sy)
    part, other = total(keep, give)
    fresh_block, coeffs, factor = finish(part, other, halves, applied, sx, sy)
    return fresh_block, coeffs.reshape(blocks, columns, columns), factor


def solution(mesh):
    placed = (P(None, None, "gz", "gx", "gy"), P("gz", "gx", "gy"), P(), P())
    return jax.shard_map(
        body,
        mesh=mesh,
        in_specs=placed,
        out_specs=(P(None, "gz", "gx", "gy"), P(), P()),
        check_vma=False,
    )
```
